32 devices in a mesh: cls: 4 (over y, x), row: 8 (over z, core).
Axes of the slice: x: 2, y: 2, z: 4, core: 2. Of those that a mesh axis runs over, the one named last changes fastest.
Arguments:
- codes: int32 [2048, 1024], P('row'), may hold values from 0 to 63
- split_feature: int32 [16, 7], P('cls'), may hold values from 0 to 1023
- split_bin: int32 [16, 7], P('cls'), may hold values from 0 to 62
- labels: int32 [2048], P('row'), may hold values from 0 to 15
- margins: float32 [2048, 16], P('row', 'cls'), may hold values from -11 to 11
Outputs:
- best_gain: float32 [16, 4], P('cls')
- leaf_value: float32 [16, 8], P('cls')
- grad_next: float32 [2048, 16], P('row', 'cls')
- hess_next: float32 [2048, 16], P('row', 'cls')
The draws below stay inside these ranges and needn't reach their ends.
All inputs are finite; a program needn't handle non-finite values.
Results may differ from the reference program's by a relative error of at most 0.0013.
Values may be sent and summed in bfloat16 or wider, within the bound.
A program may use at most 64 MiB of HBM per device.

```python
import math
import jax
import jax.numpy as jnp
from jax import lax

F = 1024
BINS = 64
LEVEL = 2
ROWS = 2048
CLASSES = 16
NODES = 4
NTOT = 7


def draw_margins(key, part):
    noise_key = jax.random.fold_in(key, 11)
    offset_key = jax.random.fold_in(key, 23)
    ramp = 1.0 + 2.0 * jnp.arange(ROWS, dtype=jnp.float32) / ROWS
    noise = jnp.clip(jax.random.normal(noise_key, (ROWS, CLASSES), jnp.float32), -4.0, 4.0)
    offset = jax.random.uniform(offset_key, (CLASSES,), jnp.float32, -2.0, 2.0)
    return noise + offset[None, :] * ramp[:, None]


def with_ends(drawn, rng, low, high):
    longest = drawn.shape.index(max(drawn.shape))
    spots = []
    for shift in (0, 1):
        where = [jax.random.randint(jax.random.fold_in(rng, axis), (), 0, length) for axis, length in enumerate(drawn.shape)]
        where[longest] = (where[longest] + shift) % drawn.shape[longest]
        spots.append(tuple(where))
    return drawn.at[spots[0]].set(low).at[spots[1]].set(high)


def setup_inputs(seed: int = 0) -> dict:
    arg_keys = jax.random.split(jax.random.key(seed), 6)
    return {
        "codes": with_ends(jax.random.randint(arg_keys[0], (ROWS, F), 0, BINS), jax.random.fold_in(arg_keys[0], 1), 0, BINS - 1).astype(jnp.int32),
        "split_feature": with_ends(jax.random.randint(arg_keys[1], (CLASSES, NTOT), 0, F), jax.random.fold_in(arg_keys[1], 1), 0, F - 1).astype(jnp.int32),
        "split_bin": with_ends(jax.random.randint(arg_keys[2], (CLASSES, NTOT), 0, BINS - 1), jax.random.fold_in(arg_keys[2], 1), 0, (BINS - 1) - 1).astype(jnp.int32),
        "labels": with_ends(jax.random.randint(arg_keys[3], (ROWS,), 0, CLASSES), jax.random.fold_in(arg_keys[3], 1), 0, CLASSES - 1).astype(jnp.int32),
        "margins": draw_margins(jax.random.fold_in(arg_keys[5], 71), 0),
    }


reg_weight = 1.0
shrink_rate = 0.3


def class_stats(margins, labels):
    expon = jnp.exp(margins)
    totals = jnp.sum(expon, axis=1, keepdims=True)
    probab = expon / totals
    target = (labels[:, None] == jnp.arange(CLASSES, dtype=jnp.int32)[None, :]).astype(jnp.float32)
    return probab - target, 2.0 * probab * (1.0 - probab)


def lookup(table, node_index):
    return jnp.take_along_axis(table.T, node_index, axis=0)


def reference(codes, split_feature, split_bin, labels, margins):
    grad, hess = class_stats(margins, labels)
    grad_low = grad.astype(jnp.bfloat16)
    hess_low = hess.astype(jnp.bfloat16)
    node_index = jnp.zeros((ROWS, CLASSES), jnp.int32)
    for level in range(LEVEL):
        feature = lookup(split_feature, node_index)
        code_here = jnp.take_along_axis(codes, feature, axis=1)
        node_index = jnp.where(code_here <= lookup(split_bin, node_index), 2 * node_index + 1, 2 * node_index + 2)
    local_node = node_index - (NODES - 1)
    member = (local_node[:, :, None] == jnp.arange(NODES, dtype=jnp.int32)[None, None, :]).astype(jnp.float32)
    stacked = jnp.stack([grad_low.astype(jnp.float32), hess_low.astype(jnp.float32)])
    weights_rows = (stacked[:, :, :, None] * member[None]).transpose(0, 2, 3, 1).reshape(2 * CLASSES * NODES, ROWS)
    block = math.gcd(F, 16)

    def feature_block(index):
        sub_codes = lax.dynamic_slice_in_dim(codes, index * block, block, 1)
        onehot = (sub_codes[:, :, None] == jnp.arange(BINS, dtype=jnp.int32)[None, None, :]).astype(jnp.float32)
        onehot = onehot.reshape(ROWS, block * BINS)
        return jnp.dot(weights_rows, onehot, precision=lax.Precision.HIGHEST, preferred_element_type=jnp.float32)

    blocks = lax.map(feature_block, jnp.arange(F // block, dtype=jnp.int32))
    hist = blocks.reshape(F // block, 2, CLASSES, NODES, block, BINS).transpose(1, 2, 3, 0, 4, 5)
    hist = hist.reshape(2, CLASSES, NODES, F, BINS)
    cumul = jnp.cumsum(hist, axis=-1)
    g_left = cumul[0, :, :, :, :-1]
    h_left = cumul[1, :, :, :, :-1]
    g_all = cumul[0, :, :, :, -1:]
    h_all = cumul[1, :, :, :, -1:]
    gain = g_left * g_left / (h_left + reg_weight) + (g_all - g_left) ** 2 / (h_all - h_left + reg_weight) - g_all * g_all / (h_all + reg_weight)
    best_gain = jnp.max(gain / (h_all + reg_weight), axis=(2, 3))
    leaf_feat = split_feature[:, NODES - 1:]
    leaf_bin = split_bin[:, NODES - 1:]
    chosen = jnp.take_along_axis(hist, leaf_feat[None, :, :, None, None], axis=3)[:, :, :, 0, :]
    below = (jnp.arange(BINS, dtype=jnp.int32)[None, None, :] <= leaf_bin[:, :, None]).astype(jnp.float32)
    left_sum = jnp.sum(chosen * below[None], axis=-1)
    right_sum = jnp.sum(chosen * (1.0 - below[None]), axis=-1)
    left_value = -shrink_rate * left_sum[0] / (left_sum[1] + reg_weight)
    right_value = -shrink_rate * right_sum[0] / (right_sum[1] + reg_weight)
    leaf_value = jnp.stack([left_value, right_value], axis=-1).reshape(CLASSES, 2 * NODES)
    final_feat = lookup(split_feature, node_index)
    code_last = jnp.take_along_axis(codes, final_feat, axis=1)
    side = (code_last > lookup(split_bin, node_index)).astype(jnp.int32)
    leaf_index = 2 * local_node + side
    update = jnp.take_along_axis(leaf_value.T, leaf_index, axis=0)
    grad_next, hess_next = class_stats(margins + update, labels)
    return best_gain, leaf_value, grad_next, hess_next
```

```python
import functools
import jax
import jax.numpy as jnp
from jax import lax
from jax.experimental import pallas as pl
from jax.experimental.pallas import tpu as pltpu
from jax.sharding import PartitionSpec as P

BINS = 64
REG = 1.0
SHRINK = 0.3
LANES = 128
FIXED = 2978.0
MESH = pl.DeviceIdType.MESH


def flip(at, bits):
    bit = 1
    while bit <= bits:
        if bits & bit:
            at = at + bit - 2 * bit * lax.rem(lax.div(at, bit), 2)
        bit *= 2
    return at


def kernel(dims, codes_in, sf_in, sb_in, lab_in, mar_in, bg_ref, lv_ref, gn_ref, hn_ref,
           codes_ref, sf_ref, sb_ref, lab_ref, mar_ref, sel, picked, csend, crecv, blocks, marg, tags, wts, le,
           acc, lsum, gsend, grecv,
           in_s, blk_s, blk_r, core_s, core_r, cod_s, cod_r, g_s, g_r):
    nc, nr, C, Rl, F, NT = dims
    CT, R, pairs = C * nc, Rl * nr, nr // 2
    nodes = (NT + 1) // 2
    leaves = 2 * nodes
    levels = nodes.bit_length() - 1
    fq = F // nc
    fb = fq // nr
    G = LANES // fb
    RG = Rl // G
    halves = Rl // LANES
    K = 2 * Rl
    N = fb * BINS
    f32, bf16, i32 = jnp.float32, jnp.bfloat16, jnp.int32
    c = lax.axis_index("cls")
    r = lax.axis_index("row")
    cls_at = [flip(c, k) for k in range(nc)]
    row_at = [flip(r, k) for k in range(nr)]

    def peer(kc, j):
        return (cls_at[kc], row_at[j])

    loads = [pltpu.make_async_copy(src, dst, in_s.at[i]) for i, (src, dst) in enumerate(
        [(codes_in, codes_ref), (sf_in, sf_ref), (sb_in, sb_ref), (lab_in, lab_ref), (mar_in, mar_ref)])]
    loads[0].start()
    loads[1].start()
    barrier = pltpu.get_barrier_semaphore()
    greet = [(kc, j) for j in range(nr - 1, -1, -1) for kc in range(nc - 1, -1, -1)
             if kc + j > 0 and (kc == 0 or j % 2 == 0)]
    for kc, j in greet:
        pl.semaphore_signal(barrier, inc=1, device_id=peer(kc, j), device_id_type=MESH)
    for d in loads[2:]:
        d.start()
    loads[1].wait()

    lane = lax.broadcasted_iota(i32, (C, F), 1)
    sel[...] = jnp.zeros_like(sel)
    for n in range(NT):
        sel[n * C:(n + 1) * C, :] = jnp.where(lane == sf_ref[:, n:n + 1], 1.0, 0.0).astype(f32)
    for d in [loads[0]] + loads[2:]:
        d.wait()
    low = codes_ref[...].astype(f32).astype(bf16)
    picked[...] = lax.dot_general(sel[...].astype(bf16), low, (((1,), (1,)), ((), ())),
                                  preferred_element_type=f32)
    bins = sb_ref[...].astype(f32)
    at = jnp.zeros((C, Rl), i32)
    for level in range(levels + 1):
        first = 2 ** level - 1
        code = picked[first * C:(first + 1) * C, :]
        cut = jnp.broadcast_to(bins[:, first:first + 1], (C, Rl))
        for j in range(1, 2 ** level):
            n = first + j
            hit = at == j
            code = jnp.where(hit, picked[n * C:(n + 1) * C, :], code)
            cut = jnp.where(hit, bins[:, n:n + 1], cut)
        at = 2 * at + jnp.where(code > cut, 1, 0)
    ids = c * C + lax.broadcasted_iota(i32, (C, Rl), 0)
    tag = at + jnp.where(lab_ref[...] == ids, leaves, 0)
    fixed = jnp.round(mar_ref[...] * FIXED).astype(i32)
    pieces = [x[:, h * LANES:(h + 1) * LANES] for x in (fixed, tag) for h in range(halves)]
    blocks[0, 0, 0] = jnp.concatenate(pieces, axis=0).astype(jnp.int16)

    pl.semaphore_wait(barrier, len(greet))

    def copy(src, dst, ss, rs, to):
        return pltpu.make_async_remote_copy(src_ref=src, dst_ref=dst, send_sem=ss, recv_sem=rs,
                                            device_id=to, device_id_type=MESH)

    own = blocks.at[0, 0, 0]
    for k in range(pairs - 1, -1, -1):
        for kc in range(nc - 1, -1, -1):
            if k + kc:
                copy(own, blocks.at[k, 0, kc], blk_s.at[k], blk_r.at[k], peer(kc, 2 * k)).start()

    def direct(k):
        part = blocks.at[0, 0, pl.ds(1, nc - 1)] if k == 0 else blocks.at[k, 0]
        return copy(part, part, blk_s.at[k], blk_r.at[k], peer(1, 0))

    forward = [copy(blocks.at[k, 0], blocks.at[k, 1], core_s.at[k], core_r.at[k], peer(0, 1)) for k in range(pairs)]

    block_of = lax.broadcasted_iota(i32, (RG, LANES), 1) // fb
    per = LANES // fb
    for t in range(fq // LANES):
        strip = codes_ref[:, pl.ds(pl.multiple_of(c * fq + t * LANES, LANES), LANES)].astype(f32)
        for jj in range(per):
            made = None
            for g in range(G):
                part = strip[g * RG:(g + 1) * RG, :]
                shift = ((g - jj) * fb) % LANES
                part = pltpu.roll(part, shift, 1) if shift else part
                made = part if made is None else jnp.where(block_of == g, part, made)
            csend[t * per + jj] = made.astype(bf16)
    cods = {j: copy(csend.at[row_at[j]], crecv.at[j], cod_s.at[j], cod_r.at[j], peer(0, j)) for j in range(1, nr)}
    for j in range(nr - 1, 0, -1):
        cods[j].start()
    crecv[0] = csend[r]

    spread_in = lax.broadcasted_iota(i32, (LANES, G * LANES), 0)
    spread_out = lax.broadcasted_iota(i32, (LANES, G * LANES), 1)
    spread = jnp.where(spread_in == (spread_out // LANES) * fb + lax.rem(spread_out, fb), 1.0, 0.0).astype(f32).astype(bf16)
    step_bin = lax.broadcasted_iota(i32, (16, LANES), 1) // fb
    zero, one = jnp.zeros((), bf16), jnp.ones((), bf16)

    def thresholds(k):
        for j in (2 * k, 2 * k + 1):
            if j:
                cods[j].wait_recv()
        packed = crecv[2 * k:2 * k + 2].reshape(2 * RG, LANES)
        wide = jnp.dot(packed, spread, preferred_element_type=f32).astype(bf16)
        for s in range(2):
            for g in range(G):
                code = wide[s * RG:(s + 1) * RG, g * LANES:(g + 1) * LANES]
                row0 = k * K + s * Rl + g * RG
                for t in range(N // LANES):
                    step = (jnp.minimum(step_bin + t * G, BINS - 2) + 1).astype(f32).astype(bf16)
                    step = jnp.broadcast_to(step[0:1, :], (RG, LANES))
                    le[row0:row0 + RG, t * LANES:(t + 1) * LANES] = jnp.clip(step - code, zero, one)

    def stats(k, start):
        for s in range(2):
            for kc in range(nc):
                both = blocks[k, s, kc].astype(i32).astype(f32)
                for h in range(halves):
                    lanes = slice(k * K + s * Rl + h * LANES, k * K + s * Rl + (h + 1) * LANES)
                    marg[kc * C:(kc + 1) * C, lanes] = both[h * C:(h + 1) * C, :]
                    tags[kc * C:(kc + 1) * C, lanes] = both[(halves + h) * C:(halves + h + 1) * C, :]
        here = slice(k * K, (k + 1) * K)
        expon = jnp.exp(marg[:, here] * (1.0 / FIXED))
        tag_all = tags[:, here]
        target = jnp.where(tag_all >= leaves, 1.0, 0.0).astype(f32)
        leaf = tag_all - leaves * target
        probab = expon * (1.0 / jnp.sum(expon, axis=0, keepdims=True))
        grad = (probab - target).astype(bf16).astype(f32)
        hess = (2.0 * probab * (1.0 - probab)).astype(bf16).astype(f32)

        def fold(x):
            total = x[:, 0:LANES]
            for i in range(1, K // LANES):
                total = total + x[:, i * LANES:(i + 1) * LANES]
            return total

        for n in range(nodes):
            sums = []
            for s in range(2):
                hit = leaf == float(2 * n + s)
                gs = jnp.where(hit, grad, 0.0)
                hs = jnp.where(hit, hess, 0.0)
                for i, x in ((2 * n + s, gs), (leaves + 2 * n + s, hs)):
                    lsum[i] = fold(x) if start else lsum[i] + fold(x)
                sums.append((gs, hs))
            wts[n * CT:(n + 1) * CT, here] = (sums[0][0] + sums[1][0]).astype(bf16)
            wts[(nodes + n) * CT:(nodes + n + 1) * CT, here] = (sums[0][1] + sums[1][1]).astype(bf16)

    width = min(512, N)

    def product(k, i):
        here = slice(k * K, (k + 1) * K)
        return jnp.dot(wts[:, here], le[here, i * width:(i + 1) * width], preferred_element_type=f32)

    order = list(range(pairs))
    direct(order[0]).wait_recv()
    forward[order[0]].start()
    for i, k in enumerate(order):
        thresholds(k)
        if i + 1 < pairs:
            direct(order[i + 1]).wait_recv()
            forward[order[i + 1]].start()
        forward[k].wait_recv()
        stats(k, i == 0)
        if i + 1 < pairs:
            for m in range(N // width):
                cols = slice(m * width, (m + 1) * width)
                if i == 0:
                    acc[:, cols] = product(k, m)
                else:
                    acc[:, cols] += product(k, m)

    g_leaf = [jnp.sum(lsum[l], axis=1, keepdims=True) for l in range(leaves)]
    h_leaf = [jnp.sum(lsum[leaves + l], axis=1, keepdims=True) for l in range(leaves)]
    values = [-SHRINK * g / (h + REG) for g, h in zip(g_leaf, h_leaf)]
    g_all = [g_leaf[2 * n] + g_leaf[2 * n + 1] for n in range(nodes)]
    h_all = [h_leaf[2 * n] + h_leaf[2 * n + 1] for n in range(nodes)]

    best = [None] * nodes
    for m in range(N // width):
        sums = product(order[-1], m)
        if pairs > 1:
            sums = sums + acc[:, m * width:(m + 1) * width]
        for n in range(nodes):
            gl = sums[n * CT:(n + 1) * CT, :]
            hl = sums[(nodes + n) * CT:(nodes + n + 1) * CT, :]
            gr = g_all[n] - gl
            hr = h_all[n] - hl + REG
            hl = hl + REG
            gain = (gl * gl * hr + gr * gr * hl) / (hl * hr)
            best[n] = gain if best[n] is None else jnp.maximum(best[n], gain)

    spot = lax.broadcasted_iota(i32, (CT, LANES), 1)
    place = lax.rem(lax.broadcasted_iota(i32, (CT, LANES), 0), C) * nodes
    tops = jnp.zeros((CT, LANES), f32)
    for n in range(nodes):
        top = jnp.max(best[n], axis=1, keepdims=True)
        den = h_all[n] + REG
        top = (top - g_all[n] * g_all[n] / den) / den
        tops = jnp.where(spot == place + n, top, tops)
    for a in range(nc):
        gsend[a] = jnp.sum(tops[a * C:(a + 1) * C, :], axis=0, keepdims=True)

    far = [(kc, j) for j in range(nr - 1, -1, -1) for kc in range(nc - 1, -1, -1) if kc + j > 0]
    for kc, j in far:
        copy(gsend.at[kc], grecv.at[kc * nr + j], g_s, g_r, peer(kc, j)).start()
    grecv[0] = gsend[0]

    tag_own = tags[:, 0:Rl]
    target_own = jnp.where(tag_own >= leaves, 1.0, 0.0).astype(f32)
    leaf_own = tag_own - leaves * target_own
    update = jnp.zeros((CT, Rl), f32)
    for l in range(leaves):
        update = jnp.where(leaf_own == float(l), values[l], update)
    expon2 = jnp.exp(marg[:, 0:Rl] * (1.0 / FIXED) + update)
    prob2 = expon2 / jnp.sum(expon2, axis=0, keepdims=True)
    gn_ref[...] = (prob2 - target_own)[0:C, :]
    hn_ref[...] = (2.0 * prob2 * (1.0 - prob2))[0:C, :]
    for l in range(leaves):
        lv_ref[:, l:l + 1] = values[l][0:C, :]

    for k in range(pairs):
        direct(k).wait_send()
        forward[k].wait_send()
    for d in cods.values():
        d.wait_send()
    every = grecv.at[pl.ds(1, nc * nr - 1)]
    whole = copy(every, every, g_s, g_r, peer(*far[0]))
    whole.wait_recv()
    top = jnp.max(grecv[...], axis=0)
    for i in range(C):
        line = pltpu.roll(top, (LANES - i * nodes) % LANES, 1) if i else top
        bg_ref[i:i + 1, :] = line[:, 0:nodes]
    whole.wait_send()


def put(a, b, c, d, oa, ob, oc, od, sems):
    copies = [pltpu.make_async_copy(x, y, sems.at[i])
              for i, (x, y) in enumerate([(a, oa), (b, ob), (c, oc), (d, od)])]
    for x in copies:
        x.start()
    for x in copies:
        x.wait()


def local(codes, split_feature, split_bin, labels, margins):
    Rl, F = codes.shape
    C, NT = split_feature.shape
    nc, nr = lax.axis_size("cls"), lax.axis_size("row")
    nodes = (NT + 1) // 2
    CT, R, pairs = C * nc, Rl * nr, nr // 2
    fb = F // (nc * nr)
    RG = Rl * fb // LANES
    f32, bf16 = jnp.float32, jnp.bfloat16
    pad = -(-NT * C // 16) * 16
    dma = pltpu.SemaphoreType.DMA
    vmem = pl.BlockSpec(memory_space=pltpu.VMEM)
    hbm = pl.BlockSpec(memory_space=pltpu.HBM)
    shapes = (jax.ShapeDtypeStruct((C, nodes), f32), jax.ShapeDtypeStruct((C, 2 * nodes), f32),
              jax.ShapeDtypeStruct((C, Rl), f32), jax.ShapeDtypeStruct((C, Rl), f32))
    made = pl.pallas_call(
        functools.partial(kernel, (nc, nr, C, Rl, F, NT)),
        out_shape=shapes,
        in_specs=[hbm] * 5,
        out_specs=(vmem,) * 4,
        scratch_shapes=[
            pltpu.VMEM((Rl, F), jnp.int32), pltpu.VMEM((C, NT), jnp.int32), pltpu.VMEM((C, NT), jnp.int32),
            pltpu.VMEM((1, Rl), jnp.int32), pltpu.VMEM((C, Rl), f32),
            pltpu.VMEM((pad, F), f32), pltpu.VMEM((pad, Rl), f32),
            pltpu.VMEM((nr, RG, LANES), bf16), pltpu.VMEM((nr, RG, LANES), bf16),
            pltpu.VMEM((pairs, 2, nc, 2 * C * Rl // LANES, LANES), jnp.int16),
            pltpu.VMEM((CT, R), f32), pltpu.VMEM((CT, R), f32),
            pltpu.VMEM((2 * nodes * CT, R), bf16),
            pltpu.VMEM((R, fb * BINS), bf16),
            pltpu.VMEM((2 * nodes * CT, fb * BINS), f32),
            pltpu.VMEM((4 * nodes, CT, LANES), f32),
            pltpu.VMEM((nc, 1, LANES), f32), pltpu.VMEM((nc * nr, 1, LANES), f32),
            dma((5,)), dma((pairs,)), dma((pairs,)), dma((pairs,)), dma((pairs,)), dma((nr,)), dma((nr,)),
            dma(()), dma(()),
        ],
        compiler_params=pltpu.CompilerParams(
            collective_id=0, has_side_effects=True, vmem_limit_bytes=40 * 2 ** 20),
        name="boost",
    )(*[pltpu.with_memory_space_constraint(x, pltpu.HBM)
        for x in (codes, split_feature, split_bin, labels.reshape(1, Rl), margins.T)])
    best, leaf, grad, hess = pl.pallas_call(
        put, out_shape=shapes, in_specs=[vmem] * 4, out_specs=(hbm,) * 4,
        scratch_shapes=[dma((4,))], name="put",
        compiler_params=pltpu.CompilerParams(vmem_limit_bytes=2 ** 20),
    )(*made)
    return best, leaf, grad.T, hess.T


def solution(mesh):
    in_specs = (P("row", None), P("cls", None), P("cls", None), P("row"), P("row", "cls"))
    out_specs = (P("cls", None), P("cls", None), P("row", "cls"), P("row", "cls"))
    return jax.shard_map(local, mesh=mesh, in_specs=in_specs, out_specs=out_specs, check_vma=False)
```

```python
import functools
import jax
import jax.numpy as jnp
from jax import lax
from jax.experimental import pallas as pl
from jax.experimental.pallas import tpu as pltpu
from jax.sharding import PartitionSpec as P

BINS = 64
REG = 1.0
SHRINK = 0.3
LANES = 128
FIXED = 2978.0
MESH = pl.DeviceIdType.MESH


def flip(at, bits):
    bit = 1
    while bit <= bits:
        if bits & bit:
            at = at + bit - 2 * bit * lax.rem(lax.div(at, bit), 2)
        bit *= 2
    return at


def kernel(dims, codes_in, sf_in, sb_in, lab_in, mar_in, bg_ref, lv_ref, gn_ref, hn_ref,
           codes_ref, sf_ref, sb_ref, lab_ref, mar_ref, sel, picked, csend, crecv, blocks, marg, tags, wts, wide,
           acc, lsum, gsend, grecv,
           in_s, row_s, row_r, cls_s, cls_r, cod_s, cod_r, g_s, g_r):
    nc, nr, C, Rl, F, NT = dims
    CT, R, pairs = C * nc, Rl * nr, nr // 2
    nodes = (NT + 1) // 2
    leaves = 2 * nodes
    levels = nodes.bit_length() - 1
    fq = F // nc
    fb = fq // nr
    G = LANES // fb
    RG = Rl // G
    halves = Rl // LANES
    K = 2 * Rl
    N = fb * BINS
    f32, bf16, i32 = jnp.float32, jnp.bfloat16, jnp.int32
    c = lax.axis_index("cls")
    r = lax.axis_index("row")
    cls_at = [flip(c, k) for k in range(nc)]
    row_at = [flip(r, k) for k in range(nr)]

    def peer(kc, j):
        return (cls_at[kc], row_at[j])

    barrier = pltpu.get_barrier_semaphore()
    greet = [(0, j) for j in range(nr - 1, 0, -1)] + [(kc, 0) for kc in range(nc - 1, 0, -1)]
    for kc, j in greet[:nr - 2]:
        pl.semaphore_signal(barrier, inc=1, device_id=peer(kc, j), device_id_type=MESH)
    strips = [pl.ds(pl.multiple_of(cls_at[k] * fq, LANES), fq) for k in range(nc)]
    first = [pltpu.make_async_copy(sf_in, sf_ref, in_s.at[0]),
             pltpu.make_async_copy(codes_in.at[:, strips[0]], codes_ref.at[:, strips[0]], in_s.at[1])]
    later = [pltpu.make_async_copy(codes_in.at[:, strips[k]], codes_ref.at[:, strips[k]], in_s.at[1 + k])
             for k in range(1, nc)]
    later += [pltpu.make_async_copy(src, dst, in_s.at[nc + 1 + i]) for i, (src, dst) in enumerate(
        [(sb_in, sb_ref), (lab_in, lab_ref), (mar_in, mar_ref)])]
    for d in first + later:
        d.start()
    for kc, j in greet[nr - 2:]:
        pl.semaphore_signal(barrier, inc=1, device_id=peer(kc, j), device_id_type=MESH)
    first[0].wait()

    lane = lax.broadcasted_iota(i32, (C, F), 1)
    sel[...] = jnp.zeros_like(sel)
    for n in range(NT):
        sel[n * C:(n + 1) * C, :] = jnp.where(lane == sf_ref[:, n:n + 1], 1.0, 0.0).astype(f32)
    first[1].wait()
    block_of = lax.broadcasted_iota(i32, (RG, LANES), 1) // fb
    per = LANES // fb
    for t in range(fq // LANES):
        strip = codes_ref[:, pl.ds(pl.multiple_of(c * fq + t * LANES, LANES), LANES)].astype(f32)
        for jj in range(per):
            made = None
            for g in range(G):
                part = strip[g * RG:(g + 1) * RG, :]
                shift = ((g - jj) * fb) % LANES
                part = pltpu.roll(part, shift, 1) if shift else part
                made = part if made is None else jnp.where(block_of == g, part, made)
            csend[t * per + jj] = made.astype(bf16)
    for d in later:
        d.wait()
    low = codes_ref[...].astype(f32).astype(bf16)
    picked[...] = lax.dot_general(sel[...].astype(bf16), low, (((1,), (1,)), ((), ())),
                                  preferred_element_type=f32)
    bins = sb_ref[...].astype(f32)
    at = jnp.zeros((C, Rl), i32)
    for level in range(levels + 1):
        node0 = 2 ** level - 1
        code = picked[node0 * C:(node0 + 1) * C, :]
        cut = jnp.broadcast_to(bins[:, node0:node0 + 1], (C, Rl))
        for j in range(1, 2 ** level):
            n = node0 + j
            hit = at == j
            code = jnp.where(hit, picked[n * C:(n + 1) * C, :], code)
            cut = jnp.where(hit, bins[:, n:n + 1], cut)
        at = 2 * at + jnp.where(code > cut, 1, 0)
    ids = c * C + lax.broadcasted_iota(i32, (C, Rl), 0)
    tag = at + jnp.where(lab_ref[...] == ids, leaves, 0)
    fixed = jnp.round(mar_ref[...] * FIXED).astype(i32)
    pieces = [x[:, h * LANES:(h + 1) * LANES] for x in (fixed, tag) for h in range(halves)]
    blocks[0, 0, 0] = jnp.concatenate(pieces, axis=0).astype(jnp.int16)

    pl.semaphore_wait(barrier, len(greet))

    def copy(src, dst, ss, rs, to):
        return pltpu.make_async_remote_copy(src_ref=src, dst_ref=dst, send_sem=ss, recv_sem=rs,
                                            device_id=to, device_id_type=MESH)

    def slot(j, kc):
        return blocks.at[j // 2, j % 2, kc]

    rows = {j: copy(slot(0, 0), slot(j, 0), row_s.at[j], row_r.at[j], peer(0, j)) for j in range(1, nr)}
    for j in range(nr - 1, 0, -1):
        rows[j].start()

    def spread_cls(k):
        for kc in range(nc - 1, 0, -1):
            copy(blocks.at[k, :, 0], blocks.at[k, :, kc], cls_s.at[k], cls_r.at[k], peer(kc, 0)).start()

    def gathered(k):
        part = blocks.at[k, :, pl.ds(1, nc - 1)]
        return copy(part, part, cls_s.at[k], cls_r.at[k], peer(1, 0))

    crecv[0] = csend[r]

    spread_in = lax.broadcasted_iota(i32, (LANES, G * LANES), 0)
    spread_out = lax.broadcasted_iota(i32, (LANES, G * LANES), 1)
    spread = jnp.where(spread_in == (spread_out // LANES) * fb + lax.rem(spread_out, fb), 1.0, 0.0).astype(f32).astype(bf16)
    step_bin = lax.broadcasted_iota(i32, (16, LANES), 1) // fb
    zero, one = jnp.zeros((), bf16), jnp.ones((), bf16)

    def unpack(k):
        for j in (2 * k, 2 * k + 1):
            if j:
                cods[j].wait_recv()
        packed = crecv[2 * k:2 * k + 2].reshape(2 * RG, LANES)
        made = jnp.dot(packed, spread, preferred_element_type=f32).astype(bf16)
        for s in range(2):
            for g in range(G):
                row0 = k * K + s * Rl + g * RG
                wide[row0:row0 + RG, :] = made[s * RG:(s + 1) * RG, g * LANES:(g + 1) * LANES]

    def stats(k, start):
        for s in range(2):
            for kc in range(nc):
                both = blocks[k, s, kc].astype(i32).astype(f32)
                for h in range(halves):
                    lanes = slice(k * K + s * Rl + h * LANES, k * K + s * Rl + (h + 1) * LANES)
                    marg[kc * C:(kc + 1) * C, lanes] = both[h * C:(h + 1) * C, :]
                    tags[kc * C:(kc + 1) * C, lanes] = both[(halves + h) * C:(halves + h + 1) * C, :]
        here = slice(k * K, (k + 1) * K)
        expon = jnp.exp(marg[:, here] * (1.0 / FIXED))
        tag_all = tags[:, here]
        target = jnp.where(tag_all >= leaves, 1.0, 0.0).astype(f32)
        leaf = tag_all - leaves * target
        probab = expon * (1.0 / jnp.sum(expon, axis=0, keepdims=True))
        grad = (probab - target).astype(bf16).astype(f32)
        hess = (2.0 * probab * (1.0 - probab)).astype(bf16).astype(f32)

        def fold(x):
            total = x[:, 0:LANES]
            for i in range(1, K // LANES):
                total = total + x[:, i * LANES:(i + 1) * LANES]
            return total

        for n in range(nodes):
            sums = []
            for s in range(2):
                hit = leaf == float(2 * n + s)
                gs = jnp.where(hit, grad, 0.0)
                hs = jnp.where(hit, hess, 0.0)
                for i, x in ((2 * n + s, gs), (leaves + 2 * n + s, hs)):
                    lsum[i] = fold(x) if start else lsum[i] + fold(x)
                sums.append((gs, hs))
            wts[n * CT:(n + 1) * CT, here] = (sums[0][0] + sums[1][0]).astype(bf16)
            wts[(nodes + n) * CT:(nodes + n + 1) * CT, here] = (sums[0][1] + sums[1][1]).astype(bf16)

    width = min(256, N)

    def product(part, i):
        here = slice(part[0] * K, (part[-1] + 1) * K)
        code = wide[here, :]
        below = []
        for t in range(i * width // LANES, (i + 1) * width // LANES):
            step = (jnp.minimum(step_bin + t * G, BINS - 2) + 1).astype(f32).astype(bf16)
            below.append(jnp.clip(jnp.broadcast_to(step[0:1, :], code.shape) - code, zero, one))
        return jnp.dot(wts[:, here], jnp.concatenate(below, axis=1), preferred_element_type=f32)

    def multiply(part):
        for m in range(N // width):
            cols = slice(m * width, (m + 1) * width)
            if part[0] == 0:
                acc[:, cols] = product(part, m)
            else:
                acc[:, cols] += product(part, m)

    def relay(part):
        for k in part:
            for j in (2 * k, 2 * k + 1):
                if j:
                    rows[j].wait_recv()
            spread_cls(k)

    def statistics(part):
        for k in part:
            gathered(k).wait_recv()
            stats(k, k == 0)

    relay([0])
    cods = {j: copy(csend.at[row_at[j]], crecv.at[j], cod_s.at[j], cod_r.at[j], peer(0, j)) for j in range(1, nr)}
    for j in range(nr - 1, 0, -1):
        cods[j].start()
    relay([1,2,3])
    unpack(0)
    unpack(1)
    statistics([0])
    statistics([1])
    multiply([0,1])
    unpack(2)
    unpack(3)
    statistics([2])
    statistics([3])
    last = [2,3]

    g_leaf = [jnp.sum(lsum[l], axis=1, keepdims=True) for l in range(leaves)]
    h_leaf = [jnp.sum(lsum[leaves + l], axis=1, keepdims=True) for l in range(leaves)]
    values = [-SHRINK * g / (h + REG) for g, h in zip(g_leaf, h_leaf)]
    g_all = [g_leaf[2 * n] + g_leaf[2 * n + 1] for n in range(nodes)]
    h_all = [h_leaf[2 * n] + h_leaf[2 * n + 1] for n in range(nodes)]

    best = [None] * nodes
    for m in range(N // width):
        sums = product(last, m)
        if last[0]:
            sums = sums + acc[:, m * width:(m + 1) * width]
        for n in range(nodes):
            gl = sums[n * CT:(n + 1) * CT, :]
            hl = sums[(nodes + n) * CT:(nodes + n + 1) * CT, :]
            gr = g_all[n] - gl
            hr = h_all[n] - hl + REG
            hl = hl + REG
            gain = (gl * gl * hr + gr * gr * hl) / (hl * hr)
            best[n] = gain if best[n] is None else jnp.maximum(best[n], gain)

    spot = lax.broadcasted_iota(i32, (CT, LANES), 1)
    tops = jnp.zeros((CT, LANES), f32)
    for n in range(nodes):
        top = jnp.max(best[n], axis=1, keepdims=True)
        den = h_all[n] + REG
        top = (top - g_all[n] * g_all[n] / den) / den
        tops = jnp.where(spot == n, top, tops)
    for a in range(nc):
        gsend[a] = tops[a * C:(a + 1) * C, :]

    far = [(kc, j) for j in range(nr - 1, -1, -1) for kc in range(nc - 1, -1, -1) if kc + j > 0]
    for kc, j in far:
        copy(gsend.at[kc], grecv.at[kc * nr + j], g_s, g_r, peer(kc, j)).start()
    grecv[0] = gsend[0]

    tag_own = tags[:, 0:Rl]
    target_own = jnp.where(tag_own >= leaves, 1.0, 0.0).astype(f32)
    leaf_own = tag_own - leaves * target_own
    update = jnp.zeros((CT, Rl), f32)
    for l in range(leaves):
        update = jnp.where(leaf_own == float(l), values[l], update)
    expon2 = jnp.exp(marg[:, 0:Rl] * (1.0 / FIXED) + update)
    prob2 = expon2 / jnp.sum(expon2, axis=0, keepdims=True)
    gn_ref[...] = (prob2 - target_own)[0:C, :]
    hn_ref[...] = (2.0 * prob2 * (1.0 - prob2))[0:C, :]
    for l in range(leaves):
        lv_ref[:, l:l + 1] = values[l][0:C, :]

    for k in range(pairs):
        gathered(k).wait_send()
    for d in list(rows.values()) + list(cods.values()):
        d.wait_send()
    every = grecv.at[pl.ds(1, nc * nr - 1)]
    whole = copy(every, every, g_s, g_r, peer(*far[0]))
    whole.wait_recv()
    bg_ref[...] = jnp.max(grecv[...], axis=0)[:, 0:nodes]
    whole.wait_send()


def put(a, b, c, d, oa, ob, oc, od, sems):
    copies = [pltpu.make_async_copy(x, y, sems.at[i])
              for i, (x, y) in enumerate([(a, oa), (b, ob), (c, oc), (d, od)])]
    for x in copies:
        x.start()
    for x in copies:
        x.wait()


def local(codes, split_feature, split_bin, labels, margins):
    Rl, F = codes.shape
    C, NT = split_feature.shape
    nc, nr = lax.axis_size("cls"), lax.axis_size("row")
    nodes = (NT + 1) // 2
    CT, R, pairs = C * nc, Rl * nr, nr // 2
    fb = F // (nc * nr)
    RG = Rl * fb // LANES
    f32, bf16 = jnp.float32, jnp.bfloat16
    pad = -(-NT * C // 16) * 16
    dma = pltpu.SemaphoreType.DMA
    vmem = pl.BlockSpec(memory_space=pltpu.VMEM)
    hbm = pl.BlockSpec(memory_space=pltpu.HBM)
    shapes = (jax.ShapeDtypeStruct((C, nodes), f32), jax.ShapeDtypeStruct((C, 2 * nodes), f32),
              jax.ShapeDtypeStruct((C, Rl), f32), jax.ShapeDtypeStruct((C, Rl), f32))
    made = pl.pallas_call(
        functools.partial(kernel, (nc, nr, C, Rl, F, NT)),
        out_shape=shapes,
        in_specs=[hbm] * 5,
        out_specs=(vmem,) * 4,
        scratch_shapes=[
            pltpu.VMEM((Rl, F), jnp.int32), pltpu.VMEM((C, NT), jnp.int32), pltpu.VMEM((C, NT), jnp.int32),
            pltpu.VMEM((1, Rl), jnp.int32), pltpu.VMEM((C, Rl), f32),
            pltpu.VMEM((pad, F), f32), pltpu.VMEM((pad, Rl), f32),
            pltpu.VMEM((nr, RG, LANES), bf16), pltpu.VMEM((nr, RG, LANES), bf16),
            pltpu.VMEM((pairs, 2, nc, 2 * C * Rl // LANES, LANES), jnp.int16),
            pltpu.VMEM((CT, R), f32), pltpu.VMEM((CT, R), f32),
            pltpu.VMEM((2 * nodes * CT, R), bf16),
            pltpu.VMEM((R, LANES), bf16),
            pltpu.VMEM((2 * nodes * CT, fb * BINS), f32),
            pltpu.VMEM((4 * nodes, CT, LANES), f32),
            pltpu.VMEM((nc, C, LANES), f32), pltpu.VMEM((nc * nr, C, LANES), f32),
            dma((nc + 4,)), dma((nr,)), dma((nr,)), dma((nr,)), dma((nr,)), dma((nr,)), dma((nr,)),
            dma(()), dma(()),
        ],
        compiler_params=pltpu.CompilerParams(
            collective_id=0, has_side_effects=True, vmem_limit_bytes=40 * 2 ** 20),
        name="boost",
    )(*[pltpu.with_memory_space_constraint(x, pltpu.HBM)
        for x in (codes, split_feature, split_bin, labels.reshape(1, Rl), margins.T)])
    best, leaf, grad, hess = pl.pallas_call(
        put, out_shape=shapes, in_specs=[vmem] * 4, out_specs=(hbm,) * 4,
        scratch_shapes=[dma((4,))], name="put",
        compiler_params=pltpu.CompilerParams(vmem_limit_bytes=2 ** 20),
    )(*made)
    return best, leaf, grad.T, hess.T


def solution(mesh):
    in_specs = (P("row", None), P("cls", None), P("cls", None), P("row"), P("row", "cls"))
    out_specs = (P("cls", None), P("cls", None), P("row", "cls"), P("row", "cls"))
    return jax.shard_map(local, mesh=mesh, in_specs=in_specs, out_specs=out_specs, check_vma=False)
```
